32 devices in a mesh: ta: 4 (over x, core), ha: 4 (over z), wa: 2 (over y).
Axes of the slice: x: 2, y: 2, z: 4, core: 2. Of those that a mesh axis runs over, the one named last changes fastest.
Arguments:
- tokens: bfloat16 [1, 16, 32, 16, 1024], P(None, 'ta', 'ha', 'wa'), may hold values from -40 to 40
- norm_gain: float32 [4, 1024], replicated, may hold values from 0.25 to 1.75
- qkv_weight: bfloat16 [3, 1024, 3, 1024], P(None, None, None, 'ta'), may hold values from -0.1875 to 0.1875
- qk_gain: float32 [3, 2, 64], replicated, may hold values from 0.25 to 1.75
- out_weight: bfloat16 [3, 1024, 1024], P(None, 'ta'), may hold values from -0.1875 to 0.1875
- ffn_in: bfloat16 [1024, 2, 2048], P(None, None, 'ta'), may hold values from -0.1875 to 0.1875
- ffn_out: bfloat16 [2048, 1024], P('ta'), may hold values from -0.125 to 0.125
Outputs:
- layer_out: bfloat16 [1, 16, 32, 16, 1024], P(None, 'ta', 'ha', 'wa')
The draws below stay inside these ranges and needn't reach their ends.
All inputs are finite; a program needn't handle non-finite values.
Results may differ from the reference program's by a relative error of at most 0.015.
Values may be sent and summed in bfloat16 or wider, within the bound.
No kernel may reach another device: no remote copies, remote signals or barrier semaphores. Data moves between devices by JAX's collectives and lax.ppermute only.
A program may use at most 192 MiB of HBM per device.

```python
import math
import jax
import jax.numpy as jnp
from jax import lax

D = 1024
HEAD_DIM = 64
FF = 2048
CLIPS = 1
ATTN_WIDTH = 1024
FRAMES = 16
HEIGHT = 32
WIDTH = 16
N_TA = 4


def draw_tokens(key, part):
    key_entries, key_column, key_row = jax.random.split(key, 3)
    extent = (CLIPS, FRAMES, HEIGHT, WIDTH, D)
    entries = jnp.clip(jax.random.normal(key_entries, extent, jnp.float32), -4.0, 4.0)
    column_scale = jnp.exp(jax.random.uniform(key_column, (D,), jnp.float32, math.log(0.3), math.log(3.0)))
    row_scale = jnp.exp(jax.random.uniform(key_row, extent[:4] + (1,), jnp.float32, math.log(0.5), math.log(2.0)))
    return (entries * column_scale * row_scale).astype(jnp.bfloat16)


def levels(key, shape, cuts, least, high):
    loudness, own = 1.0, jax.random.fold_in(key, 6)
    for axis_at, blocks in cuts:
        heights = jnp.exp(jax.random.uniform(jax.random.fold_in(own, axis_at), (blocks,), jnp.float32, least / len(cuts), high / len(cuts)))
        loudness = loudness * jnp.repeat(heights, shape[axis_at] // blocks).reshape([-1 if axis == axis_at else 1 for axis in range(len(shape))])
    return loudness


def gaussian(key, shape, spread, bound, shards=(), dtype=jnp.bfloat16):
    result = spread * jax.random.normal(key, shape, jnp.float32)
    if shards:
        result = result * levels(key, shape, shards, -0.22, 0.18)
    return jnp.clip(result, -bound, bound).astype(dtype)


def setup_inputs(seed: int = 0) -> dict:
    streams_of = jax.random.split(jax.random.key(seed), 8)
    return {
        "tokens": draw_tokens(jax.random.fold_in(streams_of[7], 71), 0),
        "norm_gain": jnp.clip(1.0 + 0.15 * jax.random.normal(streams_of[1], (4, D), jnp.float32), 0.25, 1.75),
        "qkv_weight": gaussian(streams_of[2], (3, D, 3, ATTN_WIDTH), D ** -0.5, 0.1875, ((3, 4),)),
        "qk_gain": jnp.clip(1.0 + 0.15 * jax.random.normal(streams_of[3], (3, 2, HEAD_DIM), jnp.float32), 0.25, 1.75),
        "out_weight": gaussian(streams_of[4], (3, ATTN_WIDTH, D), ATTN_WIDTH ** -0.5, 0.1875, ((1, 4),)),
        "ffn_in": gaussian(streams_of[5], (D, 2, FF), D ** -0.5, 0.1875, ((2, 4),)),
        "ffn_out": gaussian(streams_of[6], (FF, D), FF ** -0.5, 0.125, ((0, 4),)),
    }


def rms_norm(stream, gain_row):
    return stream * lax.rsqrt(lax.optimization_barrier(jnp.mean(stream * stream, axis=-1, keepdims=True)) + 1e-06) * gain_row

def head_norm(vectors, gain_row):
    return vectors * lax.rsqrt(lax.optimization_barrier(jnp.mean(vectors * vectors, axis=-1, keepdims=True)) + 1e-06) * gain_row

def grouped_product(left, right):
    inner = left.shape[-1]
    block = inner // N_TA
    left_blocks = left.reshape(-1, N_TA, block).astype(jnp.float32)
    right_blocks = right.reshape(N_TA, block, -1).astype(jnp.float32)
    parts = jnp.einsum('rgk,gkd->grd', left_blocks, right_blocks)
    rounded = lax.optimization_barrier(parts.astype(jnp.bfloat16))
    return lax.optimization_barrier(jnp.sum(rounded.astype(jnp.float32), axis=0))

def project(normed, weight_block, gain_pair):
    extent = normed.shape
    model_width = extent[-1]
    flat_qkv = jnp.dot(normed.reshape(-1, model_width), weight_block.reshape(model_width, -1), preferred_element_type=jnp.float32)
    head_count = weight_block.shape[-1] // HEAD_DIM
    flat_qkv = flat_qkv.reshape(extent[:4] + (3, head_count, HEAD_DIM))
    queries = head_norm(flat_qkv[..., 0, :, :], gain_pair[0])
    key_rows = head_norm(flat_qkv[..., 1, :, :], gain_pair[1])
    stacked = jnp.stack([queries, key_rows, flat_qkv[..., 2, :, :]], axis=4).astype(jnp.bfloat16)
    return stacked.reshape(extent[:4] + (3, head_count * HEAD_DIM))

def attend(packed, line_axis, causal):
    extent = packed.shape
    head_count = extent[-1] // HEAD_DIM
    split_shape = extent[:4] + (head_count, HEAD_DIM)
    queries = packed[..., 0, :].reshape(split_shape).astype(jnp.float32)
    key_rows = packed[..., 1, :].reshape(split_shape).astype(jnp.float32)
    values = packed[..., 2, :].reshape(split_shape).astype(jnp.float32)
    letters = 'cfyx'
    axis_letter = letters[line_axis]
    query_spec = letters.replace(axis_letter, 'q') + 'hd'
    key_spec = letters.replace(axis_letter, 'k') + 'hd'
    score_spec = letters.replace(axis_letter, '') + 'hqk'
    scores = jnp.einsum(query_spec + ',' + key_spec + '->' + score_spec, queries, key_rows) / math.sqrt(HEAD_DIM)
    exponentials = jnp.exp(scores)
    if causal:
        places = jnp.arange(extent[line_axis])
        exponentials = jnp.where(places[:, None] >= places[None, :], exponentials, jnp.zeros_like(exponentials))
    attn_probs = (exponentials / lax.optimization_barrier(jnp.sum(exponentials, axis=-1, keepdims=True))).astype(jnp.bfloat16)
    attended = jnp.einsum(score_spec + ',' + key_spec + '->' + query_spec, attn_probs.astype(jnp.float32), values)
    return attended.reshape(extent[:4] + (extent[-1],)).astype(jnp.bfloat16)

def attention_pass(stream, gain_row, weight_block, gain_pair, out_block, line_axis, causal):
    map_dim = 2 if line_axis == 1 else 1
    normed = rms_norm(stream, gain_row).astype(jnp.bfloat16)
    blocks = jnp.moveaxis(normed, map_dim, 0)

    def one_block(tile_block):
        restored = jnp.expand_dims(tile_block, map_dim)
        packed = project(restored, weight_block, gain_pair)
        attended = attend(packed, line_axis, causal)
        all_width = attended.shape[-1]
        delta_part = grouped_product(attended.reshape(-1, all_width), out_block)
        return jnp.squeeze(delta_part.reshape(restored.shape[:4] + (out_block.shape[1],)), map_dim)
    deltas = lax.map(one_block, blocks)
    return stream + jnp.moveaxis(deltas, 0, map_dim)

def mlp_block(stream, gain_row, ffn_in, ffn_out):
    normed = rms_norm(stream, gain_row).astype(jnp.bfloat16)
    blocks = jnp.moveaxis(normed, 1, 0)
    model_width = ffn_in.shape[0]
    hidden_width = ffn_in.shape[2]

    def one_frame(frame_tokens):
        flat_tokens = frame_tokens.reshape(-1, model_width)
        both_parts = jnp.dot(flat_tokens, ffn_in.reshape(model_width, -1), preferred_element_type=jnp.float32).reshape(-1, 2, hidden_width)
        hidden = (jax.nn.silu(both_parts[:, 0]) * both_parts[:, 1]).astype(jnp.bfloat16)
        return grouped_product(hidden, ffn_out).reshape(frame_tokens.shape)
    deltas = lax.map(one_frame, blocks)
    return stream + jnp.moveaxis(deltas, 0, 1)

def reference(tokens, norm_gain, qkv_weight, qk_gain, out_weight, ffn_in, ffn_out):
    stream = tokens.astype(jnp.float32)
    for pass_index, line_axis in ((0, 3), (1, 2), (2, 1)):
        stream = attention_pass(stream, norm_gain[pass_index], qkv_weight[pass_index], qk_gain[pass_index], out_weight[pass_index], line_axis, line_axis == 1)
    stream = mlp_block(stream, norm_gain[3], ffn_in, ffn_out)
    return stream.astype(jnp.bfloat16)
```

```python
import functools
import math

import jax
import jax.numpy as jnp
from jax import lax
from jax.experimental import pallas as pl
from jax.experimental.pallas import tpu as pltpu
from jax.sharding import PartitionSpec as P

HEAD_DIM = 64
GROUP = 128
F32 = jnp.float32
BF16 = jnp.bfloat16


def vmem():
    return pl.BlockSpec(memory_space=pltpu.VMEM)


def smem():
    return pl.BlockSpec(memory_space=pltpu.SMEM)


def call(body, outs, in_specs, scratch=()):
    return pl.pallas_call(
        body,
        out_shape=outs,
        in_specs=in_specs,
        out_specs=jax.tree.map(lambda _: vmem(), outs),
        scratch_shapes=list(scratch),
        compiler_params=pltpu.CompilerParams(vmem_limit_bytes=48 * 1024 * 1024),
    )


def rms(stream, gain):
    return (
        stream * lax.rsqrt(jnp.mean(stream * stream, axis=-1, keepdims=True) + 1e-06) * gain
    ).astype(BF16)


def norm_tokens(stream, gain):
    def body(x_ref, g_ref, o_ref):
        o_ref[...] = rms(x_ref[...].astype(F32), g_ref[...])

    out = jax.ShapeDtypeStruct(stream.shape, BF16)
    return call(body, out, [vmem(), vmem()])(stream, gain)


def attention(pieces, weight, gains, place, frames, line, stride, causal):
    count = len(pieces)
    rows, width = pieces[0].shape
    local = weight.shape[1] // 3
    heads = local // HEAD_DIM
    spots = rows // frames

    def body(*refs):
        g_ref = refs[0]
        x_refs = refs[1 : 1 + count]
        w_ref, gain_ref = refs[1 + count : 3 + count]
        o_refs = refs[3 + count : 3 + 2 * count]
        q_s, k_s, v_s, o_s = refs[3 + 2 * count :]
        lane_head = lax.broadcasted_iota(jnp.int32, (local, local), 0) // HEAD_DIM
        same_head = lane_head == lax.broadcasted_iota(jnp.int32, (local, local), 1) // HEAD_DIM
        ones = jnp.where(same_head, 1.0, 0.0).astype(BF16)

        def head_norm(v, gain):
            sq = v * v
            high = sq.astype(BF16)
            low = (sq - high.astype(F32)).astype(BF16)
            total = jnp.dot(high, ones, preferred_element_type=F32) + jnp.dot(
                low, ones, preferred_element_type=F32
            )
            return v * lax.rsqrt(total * (1.0 / HEAD_DIM) + 1e-06) * gain

        for r in range(count):
            qkv = jnp.dot(x_refs[r][...], w_ref[...], preferred_element_type=F32)
            shape = (frames, spots, local)
            at = slice(r * frames, (r + 1) * frames)
            q_s[at] = head_norm(qkv[:, :local], gain_ref[0:1]).reshape(shape)
            k_s[at] = head_norm(qkv[:, local : 2 * local], gain_ref[1:2]).reshape(shape)
            v_s[at] = qkv[:, 2 * local :].reshape(shape)

        q_at = lax.broadcasted_iota(jnp.int32, (heads * GROUP, GROUP), 0) % GROUP
        k_at = lax.broadcasted_iota(jnp.int32, (heads * GROUP, GROUP), 1)
        all_frames = count * frames
        if causal:
            per = GROUP // all_frames

            def frame_of(at):
                f = at // per
                return (g_ref[0] ^ (f // frames)) * frames + f % frames

            allowed = (q_at % per == k_at % per) & (frame_of(k_at) <= frame_of(q_at))
            groups = spots // per
        else:
            full = line * stride

            def line_of(at):
                return (at // full) * stride + at % stride

            allowed = line_of(q_at) == line_of(k_at)
            groups = count * rows // GROUP
        own_head = lax.broadcasted_iota(jnp.int32, (GROUP, local), 1) // HEAD_DIM
        for c in range(groups):
            if causal:
                where = (slice(None), slice(c * per, (c + 1) * per), slice(None))
            elif spots >= GROUP:
                f, s = divmod(c * GROUP, spots)
                where = (slice(f, f + 1), slice(s, s + GROUP), slice(None))
            else:
                some = GROUP // spots
                where = (slice(c * some, (c + 1) * some), slice(None), slice(None))
            q = q_s[where].reshape(GROUP, local).astype(BF16)
            k = k_s[where].reshape(GROUP, local).astype(BF16)
            v = v_s[where].reshape(GROUP, local).astype(BF16)
            stacked = jnp.concatenate(
                [jnp.where(own_head == h, q, jnp.zeros_like(q)) for h in range(heads)], axis=0
            )
            scores = lax.dot_general(
                stacked, k, (((1,), (1,)), ((), ())), preferred_element_type=F32
            ) * (1.0 / math.sqrt(HEAD_DIM))
            weights = jnp.where(allowed, jnp.exp(scores), 0.0)
            probs = (weights / jnp.sum(weights, axis=-1, keepdims=True)).astype(BF16)
            mixed = jnp.dot(probs, v, preferred_element_type=F32)
            out = mixed[:GROUP]
            for h in range(1, heads):
                out = jnp.where(own_head == h, mixed[h * GROUP : (h + 1) * GROUP], out)
            o_s[where] = out.reshape(o_s[where].shape)
        for r in range(count):
            at = slice(r * frames, (r + 1) * frames)
            o_refs[r][...] = o_s[at].reshape(rows, local).astype(BF16)

    outs = [jax.ShapeDtypeStruct((rows, local), BF16)] * count
    scratch = [pltpu.VMEM((count * frames, spots, local), F32)] * 4
    return call(body, outs, [smem()] + [vmem()] * (count + 2), scratch)(
        place, *pieces, weight, gains
    )


def out_product(pieces, weight, stream, gain, place, keep):
    count = len(pieces)

    def body(*refs):
        g_ref = refs[0]
        x_refs = refs[1 : 1 + count]
        w_ref, s_ref, gain_ref = refs[1 + count : 4 + count]
        total = s_ref[...].astype(F32)
        for r in range(count):
            total = total + jnp.dot(
                x_refs[r][...], w_ref[g_ref[0] ^ r], preferred_element_type=F32
            )
        refs[4 + count][...] = total.astype(keep)
        if gain is not None:
            refs[5 + count][...] = rms(total, gain_ref[...])

    outs = [jax.ShapeDtypeStruct(stream.shape, keep)]
    if gain is not None:
        outs.append(jax.ShapeDtypeStruct(stream.shape, BF16))
    spare = jnp.ones((1, stream.shape[1]), F32) if gain is None else gain
    return call(body, outs, [smem()] + [vmem()] * (count + 3))(
        place, *pieces, weight, stream, spare
    )


def mlp_hidden(pieces, weight):
    count = len(pieces)
    rows = pieces[0].shape[0]
    units = weight.shape[1] // 2

    def body(*refs):
        w_ref = refs[count]
        for r in range(count):
            both = jnp.dot(refs[r][...], w_ref[...], preferred_element_type=F32)
            gate = both[:, :units]
            refs[count + 1 + r][...] = (
                gate / (1.0 + jnp.exp(-gate)) * both[:, units:]
            ).astype(BF16)

    outs = [jax.ShapeDtypeStruct((rows, units), BF16)] * count
    return call(body, outs, [vmem()] * (count + 1))(*pieces, weight)


def flip(x, size, by):
    return lax.ppermute(x, "ta", [(i, i ^ by) for i in range(size)])


def spread(own, size):
    pieces = {0: own}
    half = size // 2
    while half:
        for r in list(pieces):
            pieces[r ^ half] = flip(pieces[r], size, half)
        half //= 2
    return [pieces[r] for r in range(size)]


def exchange(pieces):
    size = len(pieces)
    return [pieces[0]] + [flip(pieces[r], size, r) for r in range(1, size)]


def local(sizes, tokens, norm_gain, qkv_weight, qk_gain, out_weight, ffn_in, ffn_out):
    ta, ha, wa = sizes
    clips, frames, rows, cols, width = tokens.shape
    place = lax.axis_index("ta").astype(jnp.int32).reshape(1)
    count = clips * frames * rows * cols
    head_count = qkv_weight.shape[-1] // HEAD_DIM
    gains = jnp.tile(qk_gain, (1, 1, head_count))
    whole_out = [lax.all_gather(out_weight[p], "ta", axis=0) for p in range(3)]
    whole_down = lax.all_gather(ffn_out, "ta", axis=0)
    norms = norm_gain[:, None, :]

    def attend(normed, p, line, stride, causal):
        weight = qkv_weight[p].reshape(width, -1)
        pieces = spread(normed, ta)
        return exchange(
            attention(pieces, weight, gains[p], place, frames, line, stride, causal)
        )

    stream = lax.all_to_all(tokens, "wa", split_axis=2, concat_axis=3, tiled=True)
    stream = stream.reshape(count, width)
    normed = norm_tokens(stream, norms[0])
    got = attend(normed, 0, cols * wa, 1, False)
    (stream,) = out_product(got, whole_out[0], stream, None, place, BF16)

    few = cols // ha
    stream = stream.reshape(frames, rows // wa, wa, ha, few, width)
    stream = stream.transpose(3, 2, 0, 1, 4, 5).reshape(ha * wa, frames, rows // wa, few, width)
    stream = lax.all_to_all(stream, ("ha", "wa"), split_axis=0, concat_axis=0, tiled=True)
    stream = stream.transpose(1, 0, 2, 3, 4).reshape(count, width)

    normed = norm_tokens(stream, norms[1])
    got = attend(normed, 1, rows * ha, few, False)
    stream, normed = out_product(got, whole_out[1], stream, norms[2], place, F32)
    got = attend(normed, 2, frames * ta, 1, True)
    stream, normed = out_product(got, whole_out[2], stream, norms[3], place, F32)
    hidden = exchange(mlp_hidden(spread(normed, ta), ffn_in.reshape(width, -1)))
    (out,) = out_product(hidden, whole_down, stream, None, place, BF16)
    out = out.reshape(clips, frames, rows * ha, few, width)
    return lax.all_to_all(out, "ha", split_axis=2, concat_axis=3, tiled=True)


def solution(mesh):
    sizes = (mesh.shape["ta"], mesh.shape["ha"], mesh.shape["wa"])
    return jax.shard_map(
        functools.partial(local, sizes),
        mesh=mesh,
        in_specs=(
            P(None, "ta", "ha", "wa", None),
            P(),
            P(None, None, None, "ta"),
            P(),
            P(None, "ta", None),
            P(None, None, "ta"),
            P("ta", None),
        ),
        out_specs=P(None, "ta", "ha", "wa", None),
        check_vma=False,
    )
```

```python
import functools
import math

import jax
import jax.numpy as jnp
from jax import lax
from jax.experimental import pallas as pl
from jax.experimental.pallas import tpu as pltpu
from jax.sharding import PartitionSpec as P

HEAD_DIM = 64
GROUP = 128
F32 = jnp.float32
BF16 = jnp.bfloat16


def vmem():
    return pl.BlockSpec(memory_space=pltpu.VMEM)


def smem():
    return pl.BlockSpec(memory_space=pltpu.SMEM)


def call(body, outs, in_specs, scratch=()):
    return pl.pallas_call(
        body,
        out_shape=outs,
        in_specs=in_specs,
        out_specs=jax.tree.map(lambda _: vmem(), outs),
        scratch_shapes=list(scratch),
        compiler_params=pltpu.CompilerParams(vmem_limit_bytes=48 * 1024 * 1024),
    )


def rms(stream, gain):
    return (
        stream * lax.rsqrt(jnp.mean(stream * stream, axis=-1, keepdims=True) + 1e-06) * gain
    ).astype(BF16)


def norm_tokens(stream, gain):
    def body(x_ref, g_ref, o_ref):
        o_ref[...] = rms(x_ref[...].astype(F32), g_ref[...])

    out = jax.ShapeDtypeStruct(stream.shape, BF16)
    return call(body, out, [vmem(), vmem()])(stream, gain)


def attention(pieces, weight, gains, place, frames, line, stride, causal):
    count = len(pieces)
    rows, width = pieces[0].shape
    local = weight.shape[1] // 3
    heads = local // HEAD_DIM
    spots = rows // frames

    def body(*refs):
        g_ref = refs[0]
        x_refs = refs[1 : 1 + count]
        w_ref, gain_ref = refs[1 + count : 3 + count]
        o_refs = refs[3 + count : 3 + 2 * count]
        q_s, k_s, v_s, o_s = refs[3 + 2 * count :]
        lane_head = lax.broadcasted_iota(jnp.int32, (local, local), 0) // HEAD_DIM
        same_head = lane_head == lax.broadcasted_iota(jnp.int32, (local, local), 1) // HEAD_DIM
        ones = jnp.where(same_head, 1.0, 0.0).astype(BF16)

        def head_norm(v, gain):
            sq = v * v
            high = sq.astype(BF16)
            low = (sq - high.astype(F32)).astype(BF16)
            total = jnp.dot(high, ones, preferred_element_type=F32) + jnp.dot(
                low, ones, preferred_element_type=F32
            )
            return v * lax.rsqrt(total * (1.0 / HEAD_DIM) + 1e-06) * gain

        for r in range(count):
            qkv = jnp.dot(x_refs[r][...], w_ref[...], preferred_element_type=F32)
            shape = (frames, spots, local)
            at = slice(r * frames, (r + 1) * frames)
            q_s[at] = head_norm(qkv[:, :local], gain_ref[0:1]).reshape(shape)
            k_s[at] = head_norm(qkv[:, local : 2 * local], gain_ref[1:2]).reshape(shape)
            v_s[at] = qkv[:, 2 * local :].reshape(shape)

        q_at = lax.broadcasted_iota(jnp.int32, (heads * GROUP, GROUP), 0) % GROUP
        k_at = lax.broadcasted_iota(jnp.int32, (heads * GROUP, GROUP), 1)
        all_frames = count * frames
        if causal:
            per = GROUP // all_frames

            def frame_of(at):
                f = at // per
                return (g_ref[0] ^ (f // frames)) * frames + f % frames

            allowed = (q_at % per == k_at % per) & (frame_of(k_at) <= frame_of(q_at))
            groups = spots // per
        else:
            full = line * stride

            def line_of(at):
                return (at // full) * stride + at % stride

            allowed = line_of(q_at) == line_of(k_at)
            groups = count * rows // GROUP
        own_head = lax.broadcasted_iota(jnp.int32, (GROUP, local), 1) // HEAD_DIM
        for c in range(groups):
            if causal:
                where = (slice(None), slice(c * per, (c + 1) * per), slice(None))
            elif spots >= GROUP:
                f, s = divmod(c * GROUP, spots)
                where = (slice(f, f + 1), slice(s, s + GROUP), slice(None))
            else:
                some = GROUP // spots
                where = (slice(c * some, (c + 1) * some), slice(None), slice(None))
            q = q_s[where].reshape(GROUP, local).astype(BF16)
            k = k_s[where].reshape(GROUP, local).astype(BF16)
            v = v_s[where].reshape(GROUP, local).astype(BF16)
            stacked = jnp.concatenate(
                [jnp.where(own_head == h, q, jnp.zeros_like(q)) for h in range(heads)], axis=0
            )
            scores = lax.dot_general(
                stacked, k, (((1,), (1,)), ((), ())), preferred_element_type=F32
            ) * (1.0 / math.sqrt(HEAD_DIM))
            weights = jnp.where(allowed, jnp.exp(scores), 0.0)
            probs = (weights / jnp.sum(weights, axis=-1, keepdims=True)).astype(BF16)
            mixed = jnp.dot(probs, v, preferred_element_type=F32)
            out = mixed[:GROUP]
            for h in range(1, heads):
                out = jnp.where(own_head == h, mixed[h * GROUP : (h + 1) * GROUP], out)
            o_s[where] = out.reshape(o_s[where].shape)
        for r in range(count):
            at = slice(r * frames, (r + 1) * frames)
            o_refs[r][...] = o_s[at].reshape(rows, local).astype(BF16)

    outs = [jax.ShapeDtypeStruct((rows, local), BF16)] * count
    scratch = [pltpu.VMEM((count * frames, spots, local), F32)] * 4
    return call(body, outs, [smem()] + [vmem()] * (count + 2), scratch)(
        place, *pieces, weight, gains
    )


def out_product(pieces, weight, stream, gain, keep):
    count = len(pieces)
    depth = pieces[0].shape[1]

    def body(*refs):
        x_refs = refs[:count]
        w_ref, s_ref, gain_ref = refs[count : 3 + count]
        total = s_ref[...].astype(F32)
        for r in range(count):
            total = total + jnp.dot(
                x_refs[r][...], w_ref[:, r].reshape(depth, -1), preferred_element_type=F32
            )
        refs[3 + count][...] = total.astype(keep)
        if gain is not None:
            refs[4 + count][...] = rms(total, gain_ref[...])

    outs = [jax.ShapeDtypeStruct(stream.shape, keep)]
    if gain is not None:
        outs.append(jax.ShapeDtypeStruct(stream.shape, BF16))
    spare = jnp.ones((1, stream.shape[1]), F32) if gain is None else gain
    return call(body, outs, [vmem()] * (count + 3))(*pieces, weight, stream, spare)


def mlp_hidden(pieces, weight):
    count = len(pieces)
    rows = pieces[0].shape[0]
    units = weight.shape[1] // 2

    def body(*refs):
        w_ref = refs[count]
        for r in range(count):
            both = jnp.dot(refs[r][...], w_ref[...], preferred_element_type=F32)
            gate = both[:, :units]
            refs[count + 1 + r][...] = (
                gate / (1.0 + jnp.exp(-gate)) * both[:, units:]
            ).astype(BF16)

    outs = [jax.ShapeDtypeStruct((rows, units), BF16)] * count
    return call(body, outs, [vmem()] * (count + 1))(*pieces, weight)


def flip(x, size, by):
    return lax.ppermute(x, "ta", [(i, i ^ by) for i in range(size)])


def spread(own, size):
    pieces = {0: own}
    half = size // 2
    while half:
        for r in list(pieces):
            pieces[r ^ half] = flip(pieces[r], size, half)
        half //= 2
    return [pieces[r] for r in range(size)]


def exchange(pieces):
    size = len(pieces)
    return [pieces[0]] + [flip(pieces[r], size, r) for r in range(1, size)]


def local(sizes, tokens, norm_gain, qkv_weight, qk_gain, out_weight, ffn_in, ffn_out):
    ta, ha, wa = sizes
    clips, frames, rows, cols, width = tokens.shape
    place = lax.axis_index("ta").astype(jnp.int32).reshape(1)
    count = clips * frames * rows * cols
    head_count = qkv_weight.shape[-1] // HEAD_DIM
    gains = jnp.tile(qk_gain, (1, 1, head_count))
    rank = lax.axis_index("ha")

    def share(weight):
        part = weight.shape[0] // ha
        return lax.dynamic_slice_in_dim(weight, rank * part, part, 0)

    def whole(parts):
        return lax.all_gather(jnp.stack(parts), "ha", axis=0)

    first = whole(spread(share(out_weight[0]), ta))
    later = jnp.concatenate([share(out_weight[1]), share(out_weight[2]), share(ffn_out)])
    norms = norm_gain[:, None, :]

    def attend(normed, p, line, stride, causal):
        weight = qkv_weight[p].reshape(width, -1)
        pieces = spread(normed, ta)
        return exchange(
            attention(pieces, weight, gains[p], place, frames, line, stride, causal)
        )

    stream = lax.all_to_all(tokens, "wa", split_axis=2, concat_axis=3, tiled=True)
    stream = stream.reshape(count, width)
    normed = norm_tokens(stream, norms[0])
    got = attend(normed, 0, cols * wa, 1, False)
    later, normed = lax.optimization_barrier((later, normed))
    later = spread(later, ta)
    step = out_weight.shape[1] // ha
    second = whole([part[:step] for part in later])
    third = whole([part[step : 2 * step] for part in later])
    down = whole([part[2 * step :] for part in later])
    (stream,) = out_product(got, first, stream, None, BF16)

    few = cols // ha
    stream = stream.reshape(frames, rows // wa, wa, ha, few, width)
    stream = stream.transpose(3, 2, 0, 1, 4, 5).reshape(ha * wa, -1, width)
    stream = lax.all_to_all(stream, ("ha", "wa"), split_axis=0, concat_axis=0, tiled=True)
    stream = stream.reshape(ha * wa, frames, rows // wa, few, width)
    stream = stream.transpose(1, 0, 2, 3, 4).reshape(count, width)

    normed = norm_tokens(stream, norms[1])
    got = attend(normed, 1, rows * ha, few, False)
    stream, normed = out_product(got, second, stream, norms[2], F32)
    got = attend(normed, 2, frames * ta, 1, True)
    stream, normed = out_product(got, third, stream, norms[3], F32)
    hidden = exchange(mlp_hidden(spread(normed, ta), ffn_in.reshape(width, -1)))
    (out,) = out_product(hidden, down, stream, None, BF16)
    out = out.reshape(frames, ha, rows, few, width).transpose(1, 0, 2, 3, 4)
    out = out.reshape(ha, -1, width)
    out = lax.all_to_all(out, "ha", split_axis=0, concat_axis=0, tiled=True)
    out = out.reshape(ha, frames, rows, few, width).transpose(1, 2, 0, 3, 4)
    return out.reshape(tokens.shape)


def solution(mesh):
    sizes = (mesh.shape["ta"], mesh.shape["ha"], mesh.shape["wa"])
    return jax.shard_map(
        functools.partial(local, sizes),
        mesh=mesh,
        in_specs=(
            P(None, "ta", "ha", "wa", None),
            P(),
            P(None, None, None, "ta"),
            P(),
            P(None, "ta", None),
            P(None, None, "ta"),
            P("ta", None),
        ),
        out_specs=P(None, "ta", "ha", "wa", None),
        check_vma=False,
    )
```

```python
import functools
import math

import jax
import jax.numpy as jnp
from jax import lax
from jax.experimental import pallas as pl
from jax.experimental.pallas import tpu as pltpu
from jax.sharding import PartitionSpec as P

HEAD_DIM = 64
GROUP = 128
F32 = jnp.float32
BF16 = jnp.bfloat16


def vmem():
    return pl.BlockSpec(memory_space=pltpu.VMEM)


def smem():
    return pl.BlockSpec(memory_space=pltpu.SMEM)


def call(body, outs, in_specs, scratch=()):
    return pl.pallas_call(
        body,
        out_shape=outs,
        in_specs=in_specs,
        out_specs=jax.tree.map(lambda _: vmem(), outs),
        scratch_shapes=list(scratch),
        compiler_params=pltpu.CompilerParams(vmem_limit_bytes=48 * 1024 * 1024),
    )


def rms(stream, gain):
    return (
        stream * lax.rsqrt(jnp.mean(stream * stream, axis=-1, keepdims=True) + 1e-06) * gain
    ).astype(BF16)


def norm_tokens(stream, gain):
    def body(x_ref, g_ref, o_ref):
        o_ref[...] = rms(x_ref[...].astype(F32), g_ref[...])

    out = jax.ShapeDtypeStruct(stream.shape, BF16)
    return call(body, out, [vmem(), vmem()])(stream, gain)


def attention(pieces, weight, gains, place, frames, line, stride, causal):
    count = len(pieces)
    rows, width = pieces[0].shape
    local = weight.shape[1] // 3
    heads = local // HEAD_DIM
    spots = rows // frames

    def body(*refs):
        g_ref = refs[0]
        x_refs = refs[1 : 1 + count]
        w_ref, gain_ref = refs[1 + count : 3 + count]
        o_refs = refs[3 + count : 3 + 2 * count]
        q_s, k_s, v_s, o_s = refs[3 + 2 * count :]
        lane_head = lax.broadcasted_iota(jnp.int32, (local, local), 0) // HEAD_DIM
        same_head = lane_head == lax.broadcasted_iota(jnp.int32, (local, local), 1) // HEAD_DIM
        ones = jnp.where(same_head, 1.0, 0.0).astype(BF16)

        def head_norm(v, gain):
            sq = v * v
            high = sq.astype(BF16)
            low = (sq - high.astype(F32)).astype(BF16)
            total = jnp.dot(high, ones, preferred_element_type=F32) + jnp.dot(
                low, ones, preferred_element_type=F32
            )
            return v * lax.rsqrt(total * (1.0 / HEAD_DIM) + 1e-06) * gain

        for r in range(count):
            qkv = jnp.dot(x_refs[r][...], w_ref[...], preferred_element_type=F32)
            shape = (frames, spots, local)
            at = slice(r * frames, (r + 1) * frames)
            q_s[at] = head_norm(qkv[:, :local], gain_ref[0:1]).reshape(shape)
            k_s[at] = head_norm(qkv[:, local : 2 * local], gain_ref[1:2]).reshape(shape)
            v_s[at] = qkv[:, 2 * local :].reshape(shape)

        q_at = lax.broadcasted_iota(jnp.int32, (heads * GROUP, GROUP), 0) % GROUP
        k_at = lax.broadcasted_iota(jnp.int32, (heads * GROUP, GROUP), 1)
        all_frames = count * frames
        if causal:
            per = GROUP // all_frames

            def frame_of(at):
                f = at // per
                return (g_ref[0] ^ (f // frames)) * frames + f % frames

            allowed = (q_at % per == k_at % per) & (frame_of(k_at) <= frame_of(q_at))
            groups = spots // per
        else:
            full = line * stride

            def line_of(at):
                return (at // full) * stride + at % stride

            allowed = line_of(q_at) == line_of(k_at)
            groups = count * rows // GROUP
        own_head = lax.broadcasted_iota(jnp.int32, (GROUP, local), 1) // HEAD_DIM
        for c in range(groups):
            if causal:
                where = (slice(None), slice(c * per, (c + 1) * per), slice(None))
            elif spots >= GROUP:
                f, s = divmod(c * GROUP, spots)
                where = (slice(f, f + 1), slice(s, s + GROUP), slice(None))
            else:
                some = GROUP // spots
                where = (slice(c * some, (c + 1) * some), slice(None), slice(None))
            q = q_s[where].reshape(GROUP, local).astype(BF16)
            k = k_s[where].reshape(GROUP, local).astype(BF16)
            v = v_s[where].reshape(GROUP, local).astype(BF16)
            stacked = jnp.concatenate(
                [jnp.where(own_head == h, q, jnp.zeros_like(q)) for h in range(heads)], axis=0
            )
            scores = lax.dot_general(
                stacked, k, (((1,), (1,)), ((), ())), preferred_element_type=F32
            ) * (1.0 / math.sqrt(HEAD_DIM))
            weights = jnp.where(allowed, jnp.exp(scores), 0.0)
            probs = (weights / jnp.sum(weights, axis=-1, keepdims=True)).astype(BF16)
            mixed = jnp.dot(probs, v, preferred_element_type=F32)
            out = mixed[:GROUP]
            for h in range(1, heads):
                out = jnp.where(own_head == h, mixed[h * GROUP : (h + 1) * GROUP], out)
            o_s[where] = out.reshape(o_s[where].shape)
        for r in range(count):
            at = slice(r * frames, (r + 1) * frames)
            o_refs[r][...] = o_s[at].reshape(rows, local).astype(BF16)

    outs = [jax.ShapeDtypeStruct((rows, local), BF16)] * count
    scratch = [pltpu.VMEM((count * frames, spots, local), F32)] * 4
    return call(body, outs, [smem()] + [vmem()] * (count + 2), scratch)(
        place, *pieces, weight, gains
    )


def out_product(pieces, weight, stream, gain, place, keep):
    count = len(pieces)

    def body(*refs):
        g_ref = refs[0]
        x_refs = refs[1 : 1 + count]
        w_ref, s_ref, gain_ref = refs[1 + count : 4 + count]
        total = s_ref[...].astype(F32)
        for r in range(count):
            total = total + jnp.dot(
                x_refs[r][...], w_ref[g_ref[0] ^ r], preferred_element_type=F32
            )
        refs[4 + count][...] = total.astype(keep)
        if gain is not None:
            refs[5 + count][...] = rms(total, gain_ref[...])

    outs = [jax.ShapeDtypeStruct(stream.shape, keep)]
    if gain is not None:
        outs.append(jax.ShapeDtypeStruct(stream.shape, BF16))
    spare = jnp.ones((1, stream.shape[1]), F32) if gain is None else gain
    return call(body, outs, [smem()] + [vmem()] * (count + 3))(
        place, *pieces, weight, stream, spare
    )


def mlp_hidden(pieces, weight):
    count = len(pieces)
    rows = pieces[0].shape[0]
    units = weight.shape[1] // 2

    def body(*refs):
        w_ref = refs[count]
        for r in range(count):
            both = jnp.dot(refs[r][...], w_ref[...], preferred_element_type=F32)
            gate = both[:, :units]
            refs[count + 1 + r][...] = (
                gate / (1.0 + jnp.exp(-gate)) * both[:, units:]
            ).astype(BF16)

    outs = [jax.ShapeDtypeStruct((rows, units), BF16)] * count
    return call(body, outs, [vmem()] * (count + 1))(*pieces, weight)


def flip(x, size, by):
    return lax.ppermute(x, "ta", [(i, i ^ by) for i in range(size)])


def spread(own, size):
    pieces = {0: own}
    half = size // 2
    while half:
        for r in list(pieces):
            pieces[r ^ half] = flip(pieces[r], size, half)
        half //= 2
    return [pieces[r] for r in range(size)]


def exchange(pieces):
    size = len(pieces)
    return [pieces[0]] + [flip(pieces[r], size, r) for r in range(1, size)]


def local(sizes, tokens, norm_gain, qkv_weight, qk_gain, out_weight, ffn_in, ffn_out):
    ta, ha, wa = sizes
    clips, frames, rows, cols, width = tokens.shape
    place = lax.axis_index("ta").astype(jnp.int32).reshape(1)
    count = clips * frames * rows * cols
    head_count = qkv_weight.shape[-1] // HEAD_DIM
    gains = jnp.tile(qk_gain, (1, 1, head_count))
    whole_out = [lax.all_gather(out_weight[p], "ta", axis=0) for p in range(3)]
    whole_down = lax.all_gather(ffn_out, "ta", axis=0)
    norms = norm_gain[:, None, :]

    def attend(normed, p, line, stride, causal):
        weight = qkv_weight[p].reshape(width, -1)
        pieces = spread(normed, ta)
        return exchange(
            attention(pieces, weight, gains[p], place, frames, line, stride, causal)
        )

    stream = lax.all_to_all(tokens, "wa", split_axis=2, concat_axis=3, tiled=True)
    stream = stream.reshape(count, width)
    normed = norm_tokens(stream, norms[0])
    got = attend(normed, 0, cols * wa, 1, False)
    (stream,) = out_product(got, whole_out[0], stream, None, place, BF16)

    few = cols // ha
    stream = stream.reshape(frames, rows // wa, wa, ha, few, width)
    stream = stream.transpose(3, 2, 0, 1, 4, 5).reshape(ha * wa, frames, rows // wa, few, width)
    stream = lax.all_to_all(stream, ("ha", "wa"), split_axis=0, concat_axis=0, tiled=True)
    stream = stream.transpose(1, 0, 2, 3, 4).reshape(count, width)

    normed = norm_tokens(stream, norms[1])
    got = attend(normed, 1, rows * ha, few, False)
    stream, normed = out_product(got, whole_out[1], stream, norms[2], place, F32)
    got = attend(normed, 2, frames * ta, 1, True)
    stream, normed = out_product(got, whole_out[2], stream, norms[3], place, F32)
    hidden = exchange(mlp_hidden(spread(normed, ta), ffn_in.reshape(width, -1)))
    (out,) = out_product(hidden, whole_down, stream, None, place, BF16)
    out = out.reshape(frames, ha, rows, few, width).transpose(1, 0, 2, 3, 4)
    out = out.reshape(ha, -1, width)
    rank = lax.axis_index("ha")
    whole = jnp.zeros_like(out)
    for r in range(ha):
        part = lax.dynamic_slice_in_dim(out, rank ^ r, 1, 0)
        if r:
            part = lax.ppermute(part, "ha", [(i, i ^ r) for i in range(ha)])
        whole = lax.dynamic_update_slice_in_dim(whole, part, rank ^ r, 0)
    whole = whole.reshape(ha, frames, rows, few, width).transpose(1, 2, 0, 3, 4)
    return whole.reshape(tokens.shape)


def solution(mesh):
    sizes = (mesh.shape["ta"], mesh.shape["ha"], mesh.shape["wa"])
    return jax.shard_map(
        functools.partial(local, sizes),
        mesh=mesh,
        in_specs=(
            P(None, "ta", "ha", "wa", None),
            P(),
            P(None, None, None, "ta"),
            P(),
            P(None, "ta", None),
            P(None, None, "ta"),
            P("ta", None),
        ),
        out_specs=P(None, "ta", "ha", "wa", None),
        check_vma=False,
    )
```
